32 devices in a mesh: tm: 4 (over y, x), space: 8 (over z, core).
Axes of the slice: x: 2, y: 2, z: 4, core: 2. Of those that a mesh axis runs over, the one named last changes fastest.
Arguments:
- vectors: float32 [4, 2, 3, 64, 2048], P('tm', None, None, None, 'space'), may hold values from -6 to 6
- perambulators: float32 [4, 16, 2, 4096], P('tm'), may hold values from -0.75 to 0.75
- shift_steps: int32 [4], P('tm'), may hold values from 1 to 3, as said below
- spin_choice: int32 [4, 3], replicated, may hold values from 0 to 15
Outputs:
- elementals: float32 [4, 64, 2, 4096], P('tm', 'space')
- correlator: float32 [4, 4, 2], P('tm')
The draws below stay inside these ranges and needn't reach their ends.
Inputs may be any that keep to these rules, and one draw needn't show every extreme that they name: `shift_steps`: every distance from 1 to 3 is taken by at least one source timeslice. `spin_choice`: each entry is alpha 4 + beta for a pair of spin indices.
All inputs are finite; a program needn't handle non-finite values.
Results may differ from the reference program's by a relative error of at most 0.0003.
Values sent between devices are 32-bit elements; how exact they have to be, the bound alone decides.
A program may use at most 64 MiB of HBM per device.

```python
import math
import jax
import jax.numpy as jnp
from jax import lax

NVEC = 64
SPIN = 4
COMBOS = 4
NSITES = 2048
NT = 4


def draw_shift_steps(key, part):
    every_step = jnp.arange(1, NT, dtype=jnp.int32)
    extra_step = jax.random.randint(jax.random.fold_in(key, 17), (1,), 1, NT, dtype=jnp.int32)
    pooled = jnp.concatenate([every_step, extra_step], axis=0)
    return jax.random.permutation(jax.random.fold_in(key, 29), pooled).astype(jnp.int32)


def with_ends(entries, stream_key, smallest, top_value):
    index_at = [jax.random.randint(jax.random.fold_in(stream_key, axis), (), 0, length) for axis, length in enumerate(entries.shape)]
    longest = entries.shape.index(max(entries.shape))
    beside = index_at[:longest] + [(index_at[longest] + 1) % entries.shape[longest]] + index_at[longest + 1:]
    return entries.at[tuple(index_at)].set(smallest).at[tuple(beside)].set(top_value)


def shard_levels(own_key, dims, pieces, low, largest):
    factor_of = 1.0
    for axis_at, blocks in pieces:
        heights = jax.random.uniform(jax.random.fold_in(jax.random.fold_in(own_key, 6), axis_at), (blocks,), jnp.float32, low / len(pieces), largest / len(pieces))
        factor_of = factor_of * jnp.repeat(jnp.exp(heights), dims[axis_at] // blocks).reshape((-1,) + (1,) * (len(dims) - 1 - axis_at))
    return factor_of


def gaussian(stream_key, shape, spread, limit, pieces=(), kind=jnp.bfloat16):
    array = spread * jax.random.normal(stream_key, shape, jnp.float32)
    if pieces:
        array = array * shard_levels(stream_key, shape, pieces, -0.22, 0.18)
    return jnp.clip(array, -limit, limit).astype(kind)


def setup_inputs(seed: int = 0) -> dict:
    streams_of = jax.random.split(jax.random.key(seed), 5)
    return {
        "vectors": gaussian(streams_of[0], (NT, 2, 3, NVEC, NSITES), 1.0, 6.0, ((0, 4), (4, 8)), jnp.float32),
        "perambulators": gaussian(streams_of[1], (NT, SPIN * SPIN, 2, NVEC * NVEC), NVEC ** -0.5, 0.75, ((0, 4),), jnp.float32),
        "shift_steps": draw_shift_steps(jax.random.fold_in(streams_of[4], 71), 0),
        "spin_choice": with_ends(jax.random.randint(streams_of[3], (COMBOS, 3), 0, SPIN * SPIN), jax.random.fold_in(streams_of[3], 1), 0, (SPIN * SPIN) - 1).astype(jnp.int32),
    }


exact_mode = lax.Precision.HIGHEST

def complex_product(left_re, left_im, right_re, right_im):
    return (left_re * right_re - left_im * right_im, left_re * right_im + left_im * right_re)

def rotate(values, places):
    return jnp.concatenate([values[places:], values[:places]], axis=0)

def contract_first(left, right):
    return lax.dot_general(left, right, (((0,), (0,)), ((), ())), precision=exact_mode)

def inner_rows(left, right):
    return lax.dot_general(left, right, (((1,), (1,)), ((), ())), precision=exact_mode)

def complex_einsum(form, left, right):
    first = jnp.einsum(form, left[0], right[0], precision=exact_mode) - jnp.einsum(form, left[1], right[1], precision=exact_mode)
    second = jnp.einsum(form, left[0], right[1], precision=exact_mode) + jnp.einsum(form, left[1], right[0], precision=exact_mode)
    return (first, second)

def elemental_rows(vec_re, vec_im, lead_re, lead_im, first_row, row_count, factor):
    sites = vec_re.shape[1]
    nvec = vec_re.shape[2]
    block = math.gcd(row_count, 4)

    def one_block(index):
        offset = (first_row + index * block).astype(jnp.int32)
        part_re = lax.dynamic_slice_in_dim(vec_re, offset, block, 2)[:, :, :, None]
        part_im = lax.dynamic_slice_in_dim(vec_im, offset, block, 2)[:, :, :, None]
        full_re = vec_re[:, :, None, :]
        full_im = vec_im[:, :, None, :]
        one_re, one_im = complex_product(rotate(part_re, 1), rotate(part_im, 1), rotate(full_re, 2), rotate(full_im, 2))
        two_re, two_im = complex_product(rotate(part_re, 2), rotate(part_im, 2), rotate(full_re, 1), rotate(full_im, 1))
        cross_re = (one_re - two_re).reshape(3 * sites, block * nvec)
        cross_im = (one_im - two_im).reshape(3 * sites, block * nvec)
        out_re = contract_first(lead_re, cross_re) - contract_first(lead_im, cross_im)
        out_im = contract_first(lead_re, cross_im) + contract_first(lead_im, cross_re)
        stacked = jnp.stack([out_re, out_im], 0).reshape(2, nvec, block, nvec)
        return jnp.transpose(stacked, (2, 0, 1, 3)).reshape(block, 2, nvec * nvec) * factor
    result = lax.map(one_block, jnp.arange(row_count // block, dtype=jnp.int32))
    return result.reshape(row_count, 2, nvec * nvec)

def transform_rows(own, mats, nvec):
    combos = mats.shape[0]
    row_count = own.shape[0]
    elem = (own[:, 0].reshape(row_count, nvec, nvec), own[:, 1].reshape(row_count, nvec, nvec))
    first_mat = (mats[:, 0, 0].reshape(combos, nvec, nvec), mats[:, 0, 1].reshape(combos, nvec, nvec))
    third_mat = (mats[:, 2, 0].reshape(combos, nvec, nvec), mats[:, 2, 1].reshape(combos, nvec, nvec))
    half = complex_einsum('jik,slk->sjil', elem, third_mat)
    done = complex_einsum('smi,sjil->sjml', first_mat, half)
    return (done[0].reshape(combos * row_count, nvec * nvec), done[1].reshape(combos * row_count, nvec * nvec))

def pair_sum(sink_rows, trans_re, trans_im, mid_re, mid_im):
    combos = mid_re.shape[0]
    sink_count = sink_rows.shape[0]
    own_count = mid_re.shape[2]
    sink_re = sink_rows[:, 0]
    sink_im = sink_rows[:, 1]
    inner_re = (inner_rows(sink_re, trans_re) + inner_rows(sink_im, trans_im)).reshape(sink_count, combos, own_count)
    inner_im = (inner_rows(sink_re, trans_im) - inner_rows(sink_im, trans_re)).reshape(sink_count, combos, own_count)
    total_re = jnp.einsum('srj,rsj->s', mid_re, inner_re, precision=exact_mode) - jnp.einsum('srj,rsj->s', mid_im, inner_im, precision=exact_mode)
    total_im = jnp.einsum('srj,rsj->s', mid_re, inner_im, precision=exact_mode) + jnp.einsum('srj,rsj->s', mid_im, inner_re, precision=exact_mode)
    return jnp.stack([total_re, total_im], -1)

def reference(vectors, perambulators, shift_steps, spin_choice):
    factor = 1.0 / math.sqrt(24.0 * NSITES)
    corr_factor = 0.25 / (NVEC * math.sqrt(NVEC))

    def one_time(vec):
        vec_re = jnp.transpose(vec[0], (0, 2, 1))
        vec_im = jnp.transpose(vec[1], (0, 2, 1))
        lead_re = vec_re.reshape(3 * NSITES, NVEC)
        lead_im = vec_im.reshape(3 * NSITES, NVEC)
        return elemental_rows(vec_re, vec_im, lead_re, lead_im, 0, NVEC, factor)
    elementals = lax.map(one_time, vectors)
    targets = ((jnp.arange(NT, dtype=jnp.int32) + shift_steps.astype(jnp.int32)) % NT).astype(jnp.int32)
    sinks = jnp.take(elementals, targets, axis=0)

    def one_pair(packed):
        own, sink, peram = packed
        mats = peram[spin_choice]
        trans_re, trans_im = transform_rows(own, mats, NVEC)
        mid_re = mats[:, 1, 0].reshape(COMBOS, NVEC, NVEC)
        mid_im = mats[:, 1, 1].reshape(COMBOS, NVEC, NVEC)
        return pair_sum(sink, trans_re, trans_im, mid_re, mid_im) * corr_factor
    correlator = lax.map(one_pair, (elementals, sinks, perambulators))
    return (elementals, correlator)
```

```python
import functools
import math

import jax
import jax.numpy as jnp
from jax import lax
from jax.experimental import pallas as pl
from jax.experimental.pallas import tpu as pltpu
from jax.sharding import PartitionSpec as P

MESH = pl.DeviceIdType.MESH
VM = pl.BlockSpec(memory_space=pltpu.VMEM)
exact_mode = lax.Precision.HIGHEST
NT_DIMS = (((1,), (1,)), ((), ()))


def halves(x):
    top = x.astype(jnp.bfloat16)
    return top, (x - top.astype(jnp.float32)).astype(jnp.bfloat16)


def at_space(index):
    return (lax.axis_index("tm"), index)


def elementals_kernel(
    n, times, scale, v_ref, own_ref, full_ref, sink_ref,
    lead, d_hi, d_lo, keep, give, pair_in, chip_in,
    pair_send, pair_recv, chip_send, chip_recv,
    own_send, own_recv, fwd_send, fwd_recv, tm_send, tm_recv,
):
    me = lax.axis_index("space")
    tm = lax.axis_index("tm")
    chips = n // 2
    chip = me // 2
    core = me % 2
    mate = chip * 2 + 1 - core
    nvec = v_ref.shape[2]
    sites = v_ref.shape[3]
    own = nvec // n
    half = nvec // 2
    lanes = 2 * nvec
    group = 16 // own

    barrier = pltpu.get_barrier_semaphore()
    pl.semaphore_signal(barrier, inc=1, device_id=(tm, mate), device_id_type=MESH)
    for r in range(1, chips):
        pl.semaphore_signal(
            barrier, inc=1, device_id=(tm, (chip + r) % chips * 2 + core), device_id_type=MESH
        )
    for r in range(1, times):
        pl.semaphore_signal(
            barrier, inc=1, device_id=((tm + r) % times, me), device_id_type=MESH
        )
    pl.semaphore_wait(barrier, 1 + chips - 1 + times - 1)

    for kind in range(2):
        for a in range(3):
            re = v_ref[0, a]
            im = v_ref[1, a]
            if kind == 1:
                re = jnp.concatenate([re[half:], re[:half]], axis=0)
                im = jnp.concatenate([im[half:], im[:half]], axis=0)
            re_hi, re_lo = halves(re)
            im_hi, im_lo = halves(im)
            first = pl.ds(a * sites, sites)
            second = pl.ds((3 + a) * sites, sites)
            lead[kind, 0:nvec, first] = re_hi
            lead[kind, 0:nvec, second] = -im_hi
            lead[kind, nvec:lanes, first] = im_hi
            lead[kind, nvec:lanes, second] = re_hi
            lead[kind, lanes:lanes + nvec, first] = re_lo
            lead[kind, lanes:lanes + nvec, second] = -im_lo
            lead[kind, lanes + nvec:2 * lanes, first] = im_lo
            lead[kind, lanes + nvec:2 * lanes, second] = re_lo

    rows = half * own
    row_of = lax.broadcasted_iota(jnp.int32, (rows, lanes), 0) // own
    place = lax.broadcasted_iota(jnp.int32, (rows, lanes), 1) % nvec
    later = jnp.logical_or(place < half, place - half < row_of)

    def block(dest, out_ref):
        start = pl.multiple_of(dest * own, own)

        def rows_of(c, a):
            if own % 8 == 0:
                return v_ref[c, a, pl.ds(start, own), :]
            single = [v_ref[c, a, pl.ds(start + r, 1), :] for r in range(own)]
            return jnp.concatenate(single, axis=0)

        mine = [[rows_of(c, a) for a in range(3)] for c in range(2)]

        def fill(step, carry):
            base = step * group
            for side in range(2):
                got = []
                for g in range(group):
                    k = side * half + base + g
                    other = [[v_ref[c, a, pl.ds(k, 1), :] for a in range(3)] for c in range(2)]
                    cross = []
                    for a in range(3):
                        b, d = (a + 1) % 3, (a + 2) % 3
                        cross.append(
                            mine[0][b] * other[0][d] - mine[1][b] * other[1][d]
                            - (mine[0][d] * other[0][b] - mine[1][d] * other[1][b])
                        )
                    for a in range(3):
                        b, d = (a + 1) % 3, (a + 2) % 3
                        cross.append(
                            mine[0][b] * other[1][d] + mine[1][b] * other[0][d]
                            - (mine[0][d] * other[1][b] + mine[1][d] * other[0][b])
                        )
                    got.append(cross)
                at = pl.ds(pl.multiple_of(base * own, 16), 16)
                for m in range(6):
                    hi, lo = halves(jnp.concatenate([g[m] for g in got], axis=0))
                    d_hi[side, at, m * sites:(m + 1) * sites] = hi
                    d_lo[side, at, m * sites:(m + 1) * sites] = lo
            return carry

        lax.fori_loop(0, half // group, fill, 0)
        sums = []
        for side in range(2):
            kind = 1 - side
            both = lax.dot_general(
                d_hi[side], lead[kind], NT_DIMS, preferred_element_type=jnp.float32
            )
            rest = lax.dot_general(
                d_lo[side], lead[kind, 0:lanes], NT_DIMS, preferred_element_type=jnp.float32
            )
            sums.append(both[:, :lanes] + (both[:, lanes:] + rest))
        out_ref[...] = jnp.where(later, sums[1], sums[0])

    def pair_copy(s):
        return pltpu.make_async_remote_copy(
            give.at[s], pair_in.at[s], pair_send.at[s], pair_recv.at[s],
            device_id=(tm, mate), device_id_type=MESH,
        )

    def chip_copy(s):
        return pltpu.make_async_remote_copy(
            keep.at[s], chip_in.at[s], chip_send.at[s], chip_recv.at[s],
            device_id=(tm, (chip + 1 + s) % chips * 2 + core), device_id_type=MESH,
        )

    def one_chip(s, carry):
        z = (chip + 1 + s) % chips
        block(z * 2 + 1 - core, give.at[s])
        pair_copy(s).start()
        block(z * 2 + core, keep.at[s])
        pair_copy(s).wait_recv()
        keep[s] = keep[s] + pair_in[s]

        @pl.when(s < chips - 1)
        def _():
            chip_copy(s).start()

        return carry

    lax.fori_loop(0, chips, one_chip, 0)
    total = keep[chips - 1]
    for s in range(chips - 1):
        chip_copy(s).wait_recv()
        total = total + chip_in[s]
    own_ref[...] = total * scale

    def tm_copy(r):
        return pltpu.make_async_remote_copy(
            own_ref, sink_ref.at[r - 1], tm_send.at[r - 1], tm_recv.at[r - 1],
            device_id=((tm + r) % times, me), device_id_type=MESH,
        )

    def own_copy(r):
        target = mate if r == 0 else (chip + r) % chips * 2 + core
        return pltpu.make_async_remote_copy(
            own_ref, full_ref.at[me], own_send.at[r], own_recv.at[r],
            device_id=(tm, target), device_id_type=MESH,
        )

    def forward(r):
        slot = (chip + chips - r) % chips * 2 + core
        return pltpu.make_async_remote_copy(
            full_ref.at[slot], full_ref.at[slot], fwd_send.at[r - 1], fwd_recv.at[r - 1],
            device_id=(tm, mate), device_id_type=MESH,
        )

    for r in range(1, chips):
        own_copy(r).start()
    for r in range(1, times):
        tm_copy(r).start()
    own_copy(0).start()
    full_ref[me] = own_ref[...]
    for r in range(1, chips):
        own_copy(r).wait_recv()
        forward(r).start()
    for s in range(chips):
        pair_copy(s).wait_send()
    for s in range(chips - 1):
        chip_copy(s).wait_send()
    for r in range(1, times):
        tm_copy(r).wait()
    own_copy(0).wait()
    for r in range(1, chips):
        own_copy(r).wait_send()
        forward(r).wait()


def elementals(vec, n, times, scale):
    _, _, nvec, sites = vec.shape
    own, half = nvec // n, nvec // 2
    chips = n // 2
    tile = (half * own, 2 * nvec)
    f32 = jnp.float32
    dma = pltpu.SemaphoreType.DMA
    return pl.pallas_call(
        functools.partial(elementals_kernel, n, times, scale),
        out_shape=(
            jax.ShapeDtypeStruct(tile, f32),
            jax.ShapeDtypeStruct((n,) + tile, f32),
            jax.ShapeDtypeStruct((times - 1,) + tile, f32),
        ),
        in_specs=[VM],
        out_specs=(VM, VM, VM),
        scratch_shapes=[
            pltpu.VMEM((2, 4 * nvec, 6 * sites), jnp.bfloat16),
            pltpu.VMEM((2, half * own, 6 * sites), jnp.bfloat16),
            pltpu.VMEM((2, half * own, 6 * sites), jnp.bfloat16),
            pltpu.VMEM((chips,) + tile, f32),
            pltpu.VMEM((chips,) + tile, f32),
            pltpu.VMEM((chips,) + tile, f32),
            pltpu.VMEM((chips - 1,) + tile, f32),
            dma((chips,)), dma((chips,)),
            dma((chips - 1,)), dma((chips - 1,)),
            dma((chips,)), dma((chips,)),
            dma((chips - 1,)), dma((chips - 1,)),
            dma((times - 1,)), dma((times - 1,)),
        ],
        compiler_params=pltpu.CompilerParams(
            collective_id=0, has_side_effects=True, vmem_limit_bytes=60 * 1024 * 1024
        ),
        name="elementals",
    )(vec)


def sum_kernel(n, x_ref, o_ref, box, send, recv):
    me = lax.axis_index("space")
    tm = lax.axis_index("tm")
    barrier = pltpu.get_barrier_semaphore()
    for r in range(1, n):
        pl.semaphore_signal(barrier, inc=1, device_id=(tm, (me + r) % n), device_id_type=MESH)
    pl.semaphore_wait(barrier, n - 1)

    def copy(r):
        return pltpu.make_async_remote_copy(
            x_ref, box.at[r - 1], send.at[r - 1], recv.at[r - 1],
            device_id=(tm, (me + r) % n), device_id_type=MESH,
        )

    for r in range(1, n):
        copy(r).start()
    total = x_ref[...]
    for r in range(1, n):
        copy(r).wait_recv()
        total = total + box[r - 1]
    o_ref[...] = total
    for r in range(1, n):
        copy(r).wait_send()


def sum_space(x, n):
    dma = pltpu.SemaphoreType.DMA
    return pl.pallas_call(
        functools.partial(sum_kernel, n),
        out_shape=jax.ShapeDtypeStruct(x.shape, x.dtype),
        in_specs=[VM],
        out_specs=VM,
        scratch_shapes=[
            pltpu.VMEM((n - 1,) + x.shape, x.dtype), dma((n - 1,)), dma((n - 1,)),
        ],
        compiler_params=pltpu.CompilerParams(collective_id=1, has_side_effects=True),
        name="sum_space",
    )(x)


def unpack(packed):
    half, count, lanes = packed.shape
    nvec = lanes // 2
    rows = jnp.transpose(packed.reshape(half, count, 2, nvec), (1, 2, 0, 3))
    low_left, mixed = rows[..., :half], rows[..., half:]
    upper = jnp.triu(mixed, 1)
    lower = jnp.tril(mixed, -1)
    flip = lambda x: jnp.swapaxes(x, -1, -2)
    top = jnp.concatenate([upper - flip(upper), -flip(low_left)], axis=-1)
    bottom = jnp.concatenate([low_left, lower - flip(lower)], axis=-1)
    return -jnp.concatenate([top, bottom], axis=-2)


def complex_einsum(form, left, right):
    def dot(a, b):
        return jnp.einsum(form, a, b, precision=exact_mode)

    return (
        dot(left[0], right[0]) - dot(left[1], right[1]),
        dot(left[0], right[1]) + dot(left[1], right[0]),
    )


def shards(vectors, perambulators, shift_steps, spin_choice):
    vec = vectors[0]
    nvec = vec.shape[2]
    sites = vec.shape[3]
    n = lax.axis_size("space")
    times = lax.axis_size("tm")
    own = nvec // n
    scale = 1.0 / math.sqrt(24.0 * sites * n)
    corr_scale = 0.25 / (nvec * math.sqrt(nvec))
    mine, full, sinks = elementals(vec, n, times, scale)
    packed = (nvec // 2, own, 2 * nvec)
    out = unpack(mine.reshape(packed)).reshape(own, 2, nvec * nvec)
    chosen = lax.dynamic_index_in_dim(sinks, times - shift_steps[0] - 1, 0, keepdims=False)
    sink = unpack(chosen.reshape(packed))
    full = jnp.transpose(full.reshape((n,) + packed), (1, 0, 2, 3))
    whole = unpack(full.reshape(nvec // 2, nvec, 2 * nvec))
    mats = perambulators[0][spin_choice].reshape(spin_choice.shape + (2, nvec, nvec))
    first = lax.axis_index("space") * own
    mid = lax.dynamic_slice_in_dim(mats[:, 1], first, own, 2)
    two = complex_einsum("jml,slk->sjmk", (sink[:, 0], -sink[:, 1]), (mats[:, 2, 0], mats[:, 2, 1]))
    one = complex_einsum("sjmk,smi->sjik", two, (mats[:, 0, 0], mats[:, 0, 1]))
    mixed = complex_einsum("srj,jik->srik", (mid[:, 0], mid[:, 1]), (whole[:, 0], whole[:, 1]))
    corr_re = jnp.sum(mixed[0] * one[0] - mixed[1] * one[1], axis=(1, 2, 3))
    corr_im = jnp.sum(mixed[0] * one[1] + mixed[1] * one[0], axis=(1, 2, 3))
    combos = spin_choice.shape[0]
    flat = jnp.stack([corr_re, corr_im], -1) * corr_scale
    tile = jnp.zeros((8, 128), jnp.float32).at[:combos, :2].set(flat)
    correlator = sum_space(tile, n)[:combos, :2]
    return (out[None], correlator[None])


def solution(mesh):
    placed = (P("tm", None, None, None, "space"), P("tm", None, None, None), P("tm"), P())
    return jax.shard_map(
        shards,
        mesh=mesh,
        in_specs=placed,
        out_specs=(P("tm", "space", None, None), P("tm", None, None)),
        check_vma=False,
    )
```

```python
import functools
import math

import jax
import jax.numpy as jnp
from jax import lax
from jax.experimental import pallas as pl
from jax.experimental.pallas import tpu as pltpu
from jax.sharding import PartitionSpec as P

MESH = pl.DeviceIdType.MESH
VM = pl.BlockSpec(memory_space=pltpu.VMEM)
NT_DIMS = (((1,), (1,)), ((), ()))


def halves(x):
    top = x.astype(jnp.bfloat16)
    return top, (x - top.astype(jnp.float32)).astype(jnp.bfloat16)


def at_space(index):
    return (lax.axis_index("tm"), index)


def elementals_kernel(
    n, times, scale, corr_scale, v_ref, mats_ref, shift_ref, spin_ref, out_ref, corr_ref,
    own_ref, full_ref, sink_ref, lead, d_hi, d_lo, keep, give, pair_in, chip_in,
    right_hi, right_lo, half_hi, half_lo, weight, mixed_rows, chosen, tile_ref, box,
    pair_send, pair_recv, chip_send, chip_recv,
    own_send, own_recv, fwd_send, fwd_recv, tm_send, tm_recv,
    sum_send, sum_recv,
):
    me = lax.axis_index("space")
    tm = lax.axis_index("tm")
    chips = n // 2
    chip = me // 2
    core = me % 2
    mate = chip * 2 + 1 - core
    nvec = v_ref.shape[2]
    sites = v_ref.shape[3]
    own = nvec // n
    half = nvec // 2
    lanes = 2 * nvec
    group = 16 // own

    barrier = pltpu.get_barrier_semaphore()
    for r in range(1, n):
        pl.semaphore_signal(barrier, inc=1, device_id=(tm, (me + r) % n), device_id_type=MESH)
    for r in range(1, times):
        pl.semaphore_signal(
            barrier, inc=1, device_id=((tm + r) % times, me), device_id_type=MESH
        )
    pl.semaphore_wait(barrier, n - 1 + times - 1)

    for kind in range(2):
        for a in range(3):
            re = v_ref[0, a]
            im = v_ref[1, a]
            if kind == 1:
                re = jnp.concatenate([re[half:], re[:half]], axis=0)
                im = jnp.concatenate([im[half:], im[:half]], axis=0)
            re_hi, re_lo = halves(re)
            im_hi, im_lo = halves(im)
            first = pl.ds(a * sites, sites)
            second = pl.ds((3 + a) * sites, sites)
            lead[kind, 0:nvec, first] = re_hi
            lead[kind, 0:nvec, second] = -im_hi
            lead[kind, nvec:lanes, first] = im_hi
            lead[kind, nvec:lanes, second] = re_hi
            lead[kind, lanes:lanes + nvec, first] = re_lo
            lead[kind, lanes:lanes + nvec, second] = -im_lo
            lead[kind, lanes + nvec:2 * lanes, first] = im_lo
            lead[kind, lanes + nvec:2 * lanes, second] = re_lo

    rows = half * own
    row_of = lax.broadcasted_iota(jnp.int32, (rows, lanes), 0) // own
    place = lax.broadcasted_iota(jnp.int32, (rows, lanes), 1) % nvec
    later = jnp.logical_or(place < half, place - half < row_of)

    def block(dest, out_ref):
        start = pl.multiple_of(dest * own, own)

        def rows_of(c, a):
            if own % 8 == 0:
                return v_ref[c, a, pl.ds(start, own), :]
            single = [v_ref[c, a, pl.ds(start + r, 1), :] for r in range(own)]
            return jnp.concatenate(single, axis=0)

        mine = [[rows_of(c, a) for a in range(3)] for c in range(2)]

        def fill(step, carry):
            base = step * group
            for side in range(2):
                got = []
                for g in range(group):
                    k = side * half + base + g
                    other = [[v_ref[c, a, pl.ds(k, 1), :] for a in range(3)] for c in range(2)]
                    cross = []
                    for a in range(3):
                        b, d = (a + 1) % 3, (a + 2) % 3
                        cross.append(
                            mine[0][b] * other[0][d] - mine[1][b] * other[1][d]
                            - (mine[0][d] * other[0][b] - mine[1][d] * other[1][b])
                        )
                    for a in range(3):
                        b, d = (a + 1) % 3, (a + 2) % 3
                        cross.append(
                            mine[0][b] * other[1][d] + mine[1][b] * other[0][d]
                            - (mine[0][d] * other[1][b] + mine[1][d] * other[0][b])
                        )
                    got.append(cross)
                at = pl.ds(pl.multiple_of(base * own, 16), 16)
                for m in range(6):
                    hi, lo = halves(jnp.concatenate([g[m] for g in got], axis=0))
                    d_hi[side, at, m * sites:(m + 1) * sites] = hi
                    d_lo[side, at, m * sites:(m + 1) * sites] = lo
            return carry

        lax.fori_loop(0, half // group, fill, 0)
        sums = []
        for side in range(2):
            kind = 1 - side
            both = lax.dot_general(
                d_hi[side], lead[kind], NT_DIMS, preferred_element_type=jnp.float32
            )
            rest = lax.dot_general(
                d_lo[side], lead[kind, 0:lanes], NT_DIMS, preferred_element_type=jnp.float32
            )
            sums.append(both[:, :lanes] + (both[:, lanes:] + rest))
        out_ref[...] = jnp.where(later, sums[1], sums[0])

    def pair_copy(s):
        return pltpu.make_async_remote_copy(
            give.at[s], pair_in.at[s], pair_send.at[s], pair_recv.at[s],
            device_id=(tm, mate), device_id_type=MESH,
        )

    def chip_copy(s):
        return pltpu.make_async_remote_copy(
            keep.at[s], chip_in.at[s], chip_send.at[s], chip_recv.at[s],
            device_id=(tm, (chip + 1 + s) % chips * 2 + core), device_id_type=MESH,
        )

    def one_chip(s, carry):
        z = (chip + 1 + s) % chips
        block(z * 2 + 1 - core, give.at[s])
        pair_copy(s).start()
        block(z * 2 + core, keep.at[s])
        pair_copy(s).wait_recv()
        keep[s] = keep[s] + pair_in[s]

        @pl.when(s < chips - 1)
        def _():
            chip_copy(s).start()

        return carry

    lax.fori_loop(0, chips, one_chip, 0)
    total = keep[chips - 1]
    for s in range(chips - 1):
        chip_copy(s).wait_recv()
        total = total + chip_in[s]
    own_ref[...] = total * scale

    def tm_copy(r):
        return pltpu.make_async_remote_copy(
            own_ref, sink_ref.at[r - 1], tm_send.at[r - 1], tm_recv.at[r - 1],
            device_id=((tm + r) % times, me), device_id_type=MESH,
        )

    def own_copy(r):
        target = mate if r == 0 else (chip + r) % chips * 2 + core
        return pltpu.make_async_remote_copy(
            own_ref, full_ref.at[me], own_send.at[r], own_recv.at[r],
            device_id=(tm, target), device_id_type=MESH,
        )

    def forward(r):
        slot = (chip + chips - r) % chips * 2 + core
        return pltpu.make_async_remote_copy(
            full_ref.at[slot], full_ref.at[slot], fwd_send.at[r - 1], fwd_recv.at[r - 1],
            device_id=(tm, mate), device_id_type=MESH,
        )

    for r in range(1, times):
        tm_copy(r).start()
    for r in range(1, chips):
        own_copy(r).start()
    own_copy(0).start()
    full_ref[me] = own_ref[...]

    row = lax.broadcasted_iota(jnp.int32, (half, lanes), 0)
    lane = lax.broadcasted_iota(jnp.int32, (half, lanes), 1)
    spot = lane % nvec
    left = spot < half
    real = lane < nvec
    minus_plus = jnp.where(lax.broadcasted_iota(jnp.int32, (nvec, lanes), 1) < nvec, -1.0, 1.0)

    def dense(p):
        t = jnp.transpose(jnp.concatenate([p] * (lanes // half), axis=0))
        base = jnp.where(real, t[:half], t[nvec:nvec + half])
        mixed = jnp.where(real, t[half:nvec], t[nvec + half:])
        moved = pltpu.roll(p, lanes - half, 1)
        zero = jnp.zeros_like(p)
        upper = jnp.where(spot > row, moved, jnp.where(spot < row, -mixed, zero))
        lower = jnp.where(spot - half < row, p, jnp.where(spot - half > row, -mixed, zero))
        return jnp.where(left, upper, -base), jnp.where(left, p, lower)

    for j in range(own):
        top, bottom = dense(own_ref[pl.ds(j, half, stride=own), :])
        matrix = -jnp.concatenate([top, bottom], axis=0)
        out_ref[j, 0] = matrix[:, :nvec]
        out_ref[j, 1] = pltpu.roll(matrix, nvec, 1)[:, :nvec]

    combos = spin_ref.shape[0]
    for s in range(combos):
        for q in range(2):
            spins = mats_ref[spin_ref[s, 2 * q]]
            at = (s * 2 + q) * lanes
            top_hi, top_lo = halves(spins)
            low_hi, low_lo = halves(-minus_plus * pltpu.roll(spins, nvec, 1))
            right_hi[0:nvec, at:at + lanes] = top_hi
            right_lo[0:nvec, at:at + lanes] = top_lo
            right_hi[nvec:lanes, at:at + lanes] = low_hi
            right_lo[nvec:lanes, at:at + lanes] = low_lo

    def dot3(a_hi, a_lo, b_hi, b_lo):
        def dot(a, b):
            return jnp.dot(a, b, preferred_element_type=jnp.float32)

        return dot(a_hi, b_hi) + (dot(a_hi, b_lo) + dot(a_lo, b_hi))

    for r in range(1, times):
        tm_copy(r).wait_recv()
    chosen[...] = sink_ref[jnp.clip(times - 1 - shift_ref[0], 0, times - 2)]
    for j in range(own):
        top, bottom = dense(chosen[pl.ds(j, half, stride=own), :])
        hi, lo = halves(jnp.concatenate([top, bottom], axis=0))
        got = dot3(hi, lo, right_hi[...], right_lo[...])
        hi, lo = halves(got)
        for s in range(combos):
            for q in range(2):
                at = (s * 2 + q) * lanes
                where = (s, pl.ds(q * nvec, nvec), pl.ds(j * lanes, lanes))
                half_hi[where] = hi[:, at:at + lanes]
                half_lo[where] = lo[:, at:at + lanes]
    for r in range(1, chips):
        own_copy(r).wait_recv()
        forward(r).start()
    for s in range(combos):
        both = jnp.concatenate(
            [mats_ref[spin_ref[s, 2]], mats_ref[spin_ref[s, 0]]], axis=0
        )
        hi, lo = halves(jnp.transpose(both))
        got = dot3(hi, lo, half_hi[s], half_lo[s])
        for j in range(own):
            at = j * lanes
            whole = got[:nvec, at:at + lanes] + minus_plus * pltpu.roll(
                got[nvec:, at:at + lanes], nvec, 1
            )
            bent = jnp.where(
                jnp.logical_or(left, spot - half < row),
                whole[half:], pltpu.roll(whole[:half], half, 1),
            )
            weight[pl.ds((s * own + j) * half, half), :] = bent

    mid = []
    for s in range(combos):
        which = spin_ref[s, 1]
        if own % 8 == 0:
            mid.append(mats_ref[which, pl.ds(pl.multiple_of(me * own, own), own), :])
        else:
            for r in range(own):
                mid.append(mats_ref[which, pl.ds(me * own + r, 1), :])
    mid = jnp.concatenate(mid, axis=0)
    count = combos * own
    mid = jnp.concatenate([mid[:, :nvec], pltpu.roll(mid, nvec, 1)[:, :nvec]], axis=0)
    mid_hi, mid_lo = halves(mid)
    own_copy(0).wait_recv()
    for r in range(1, chips):
        forward(r).wait_recv()
    sign = jnp.where(lax.broadcasted_iota(jnp.int32, (count, lanes), 1) < nvec, -1.0, 1.0)
    for k in range(half):
        pieces = [full_ref[d, k * own:(k + 1) * own, :] for d in range(n)]
        hi, lo = halves(jnp.concatenate(pieces, axis=0))
        got = dot3(mid_hi, mid_lo, hi, lo)
        mixed_rows[pl.ds(k * count, count), :] = got[:count] + sign * pltpu.roll(got[count:], nvec, 1)

    straight, crossed = [], []
    for s in range(combos):
        one = jnp.zeros((half, lanes), jnp.float32)
        two = jnp.zeros((half, lanes), jnp.float32)
        for j in range(own):
            at = s * own + j
            value = mixed_rows[pl.ds(at, half, stride=count), :]
            factor = weight[pl.ds(at * half, half), :]
            one = one + value * factor
            two = two + value * pltpu.roll(factor, nvec, 1)
        straight.append(jnp.sum(jnp.where(real, one, -one), axis=0, keepdims=True))
        crossed.append(jnp.sum(two, axis=0, keepdims=True))
    tile_ref[...] = jnp.concatenate(straight + crossed, axis=0)

    def sum_copy(r):
        return pltpu.make_async_remote_copy(
            tile_ref, box.at[r - 1], sum_send.at[r - 1], sum_recv.at[r - 1],
            device_id=(tm, (me + r) % n), device_id_type=MESH,
        )

    for r in range(1, n):
        sum_copy(r).start()
    for s in range(chips):
        pair_copy(s).wait_send()
    for s in range(chips - 1):
        chip_copy(s).wait_send()
    for r in range(1, times):
        tm_copy(r).wait_send()
    own_copy(0).wait_send()
    for r in range(1, chips):
        own_copy(r).wait_send()
        forward(r).wait_send()
    answer = tile_ref[...]
    for r in range(1, n):
        sum_copy(r).wait_recv()
        answer = answer + box[r - 1]
    lines = jnp.sum(answer, axis=1, keepdims=True) * corr_scale
    corr_ref[...] = jnp.concatenate([lines[:combos], lines[combos:]], axis=1)
    for r in range(1, n):
        sum_copy(r).wait_send()


def shards(vectors, perambulators, shift_steps, spin_choice):
    vec = vectors[0]
    _, _, nvec, sites = vec.shape
    spin_pairs = perambulators.shape[1]
    combos = spin_choice.shape[0]
    n = lax.axis_size("space")
    times = lax.axis_size("tm")
    own, half, lanes = nvec // n, nvec // 2, 2 * nvec
    chips = n // 2
    scale = 1.0 / math.sqrt(24.0 * sites * n)
    corr_scale = 0.25 / (nvec * math.sqrt(nvec))
    mats = perambulators[0].reshape(spin_pairs, 2, nvec, nvec)
    mats = jnp.transpose(mats, (0, 2, 1, 3)).reshape(spin_pairs, nvec, lanes)
    tile = (half * own, lanes)
    f32, bf16 = jnp.float32, jnp.bfloat16
    dma = pltpu.SemaphoreType.DMA
    smem = pl.BlockSpec(memory_space=pltpu.SMEM)
    out, correlator = pl.pallas_call(
        functools.partial(elementals_kernel, n, times, scale, corr_scale),
        out_shape=(
            jax.ShapeDtypeStruct((own, 2, nvec, nvec), f32),
            jax.ShapeDtypeStruct((combos, 2), f32),
        ),
        in_specs=[VM, VM, smem, smem],
        out_specs=(VM, VM),
        scratch_shapes=[
            pltpu.VMEM(tile, f32),
            pltpu.VMEM((n,) + tile, f32),
            pltpu.VMEM((times - 1,) + tile, f32),
            pltpu.VMEM((2, 4 * nvec, 6 * sites), bf16),
            pltpu.VMEM((2, half * own, 6 * sites), bf16),
            pltpu.VMEM((2, half * own, 6 * sites), bf16),
            pltpu.VMEM((chips,) + tile, f32),
            pltpu.VMEM((chips,) + tile, f32),
            pltpu.VMEM((chips,) + tile, f32),
            pltpu.VMEM((chips - 1,) + tile, f32),
            pltpu.VMEM((lanes, combos * 2 * lanes), bf16),
            pltpu.VMEM((lanes, combos * 2 * lanes), bf16),
            pltpu.VMEM((combos, 2 * nvec, own * lanes), bf16),
            pltpu.VMEM((combos, 2 * nvec, own * lanes), bf16),
            pltpu.VMEM((combos * own * half, lanes), f32),
            pltpu.VMEM((combos * own * half, lanes), f32),
            pltpu.VMEM(tile, f32),
            pltpu.VMEM((2 * combos, lanes), f32),
            pltpu.VMEM((n - 1, 2 * combos, lanes), f32),
            dma((chips,)), dma((chips,)),
            dma((chips - 1,)), dma((chips - 1,)),
            dma((chips,)), dma((chips,)),
            dma((chips - 1,)), dma((chips - 1,)),
            dma((times - 1,)), dma((times - 1,)),
            dma((n - 1,)), dma((n - 1,)),
        ],
        compiler_params=pltpu.CompilerParams(
            collective_id=0, has_side_effects=True, vmem_limit_bytes=60 * 1024 * 1024
        ),
        name="elementals",
    )(vec, mats, shift_steps, spin_choice)
    return (out.reshape(1, own, 2, nvec * nvec), correlator[None])


def solution(mesh):
    placed = (P("tm", None, None, None, "space"), P("tm", None, None, None), P("tm"), P())
    return jax.shard_map(
        shards,
        mesh=mesh,
        in_specs=placed,
        out_specs=(P("tm", "space", None, None), P("tm", None, None)),
        check_vma=False,
    )
```

```python
import functools
import math

import jax
import jax.numpy as jnp
from jax import lax
from jax.experimental import pallas as pl
from jax.experimental.pallas import tpu as pltpu
from jax.sharding import PartitionSpec as P

MESH = pl.DeviceIdType.MESH
VM = pl.BlockSpec(memory_space=pltpu.VMEM)
NT_DIMS = (((1,), (1,)), ((), ()))


def halves(x):
    top = x.astype(jnp.bfloat16)
    return top, (x - top.astype(jnp.float32)).astype(jnp.bfloat16)


def at_space(index):
    return (lax.axis_index("tm"), index)


def elementals_kernel(
    n, times, scale, corr_scale, v_ref, mats_ref, shift_ref, spin_ref, out_ref, corr_ref,
    own_ref, full_ref, sink_ref, lead, d_hi, d_lo, keep, give, pair_in, chip_in,
    right_hi, right_lo, half_hi, half_lo, weight, mixed_rows, chosen, board, spin_mats, tile_ref, box,
    pair_send, pair_recv, chip_send, chip_recv,
    own_send, own_recv, fwd_send, fwd_recv, tm_send, tm_recv,
    sum_send, sum_recv,
):
    me = lax.axis_index("space")
    tm = lax.axis_index("tm")
    chips = n // 2
    chip = me // 2
    core = me % 2
    mate = chip * 2 + 1 - core
    nvec = v_ref.shape[2]
    sites = v_ref.shape[3]
    own = nvec // n
    half = nvec // 2
    lanes = 2 * nvec
    group = 16 // own

    barrier = pltpu.get_barrier_semaphore()
    for r in range(1, n):
        pl.semaphore_signal(barrier, inc=1, device_id=(tm, (me + r) % n), device_id_type=MESH)
    for r in range(1, times):
        pl.semaphore_signal(
            barrier, inc=1, device_id=((tm + r) % times, me), device_id_type=MESH
        )
    pl.semaphore_wait(barrier, n - 1 + times - 1)

    for kind in range(2):
        for a in range(3):
            re = v_ref[0, a]
            im = v_ref[1, a]
            if kind == 1:
                re = jnp.concatenate([re[half:], re[:half]], axis=0)
                im = jnp.concatenate([im[half:], im[:half]], axis=0)
            re_hi, re_lo = halves(re)
            im_hi, im_lo = halves(im)
            first = pl.ds(a * sites, sites)
            second = pl.ds((3 + a) * sites, sites)
            lead[kind, 0:nvec, first] = re_hi
            lead[kind, 0:nvec, second] = -im_hi
            lead[kind, nvec:lanes, first] = im_hi
            lead[kind, nvec:lanes, second] = re_hi
            lead[kind, lanes:lanes + nvec, first] = re_lo
            lead[kind, lanes:lanes + nvec, second] = -im_lo
            lead[kind, lanes + nvec:2 * lanes, first] = im_lo
            lead[kind, lanes + nvec:2 * lanes, second] = re_lo

    rows = half * own
    row_of = lax.broadcasted_iota(jnp.int32, (rows, lanes), 0) // own
    place = lax.broadcasted_iota(jnp.int32, (rows, lanes), 1) % nvec
    later = jnp.logical_or(place < half, place - half < row_of)

    def block(dest, out_ref):
        start = pl.multiple_of(dest * own, own)

        def rows_of(c, a):
            if own % 8 == 0:
                return v_ref[c, a, pl.ds(start, own), :]
            single = [v_ref[c, a, pl.ds(start + r, 1), :] for r in range(own)]
            return jnp.concatenate(single, axis=0)

        mine = [[rows_of(c, a) for a in range(3)] for c in range(2)]

        def fill(step, carry):
            base = step * group
            for side in range(2):
                got = []
                for g in range(group):
                    k = side * half + base + g
                    other = [[v_ref[c, a, pl.ds(k, 1), :] for a in range(3)] for c in range(2)]
                    cross = []
                    for a in range(3):
                        b, d = (a + 1) % 3, (a + 2) % 3
                        cross.append(
                            mine[0][b] * other[0][d] - mine[1][b] * other[1][d]
                            - (mine[0][d] * other[0][b] - mine[1][d] * other[1][b])
                        )
                    for a in range(3):
                        b, d = (a + 1) % 3, (a + 2) % 3
                        cross.append(
                            mine[0][b] * other[1][d] + mine[1][b] * other[0][d]
                            - (mine[0][d] * other[1][b] + mine[1][d] * other[0][b])
                        )
                    got.append(cross)
                at = pl.ds(pl.multiple_of(base * own, 16), 16)
                for m in range(6):
                    hi, lo = halves(jnp.concatenate([g[m] for g in got], axis=0))
                    d_hi[side, at, m * sites:(m + 1) * sites] = hi
                    d_lo[side, at, m * sites:(m + 1) * sites] = lo
            return carry

        lax.fori_loop(0, half // group, fill, 0)
        sums = []
        for side in range(2):
            kind = 1 - side
            both = lax.dot_general(
                d_hi[side], lead[kind], NT_DIMS, preferred_element_type=jnp.float32
            )
            rest = lax.dot_general(
                d_lo[side], lead[kind, 0:lanes], NT_DIMS, preferred_element_type=jnp.float32
            )
            sums.append(both[:, :lanes] + (both[:, lanes:] + rest))
        out_ref[...] = jnp.where(later, sums[1], sums[0])

    def pair_copy(s):
        return pltpu.make_async_remote_copy(
            give.at[s], pair_in.at[s], pair_send.at[s], pair_recv.at[s],
            device_id=(tm, mate), device_id_type=MESH,
        )

    def chip_copy(s):
        return pltpu.make_async_remote_copy(
            keep.at[s], chip_in.at[s], chip_send.at[s], chip_recv.at[s],
            device_id=(tm, (chip + 1 + s) % chips * 2 + core), device_id_type=MESH,
        )

    def one_chip(s, carry):
        z = (chip + 1 + s) % chips
        block(z * 2 + 1 - core, give.at[s])
        pair_copy(s).start()
        block(z * 2 + core, keep.at[s])
        pair_copy(s).wait_recv()
        keep[s] = keep[s] + pair_in[s]

        @pl.when(s < chips - 1)
        def _():
            chip_copy(s).start()

        return carry

    lax.fori_loop(0, chips, one_chip, 0)
    total = keep[chips - 1]
    for s in range(chips - 1):
        chip_copy(s).wait_recv()
        total = total + chip_in[s]
    own_ref[...] = total * scale

    def tm_copy(r):
        return pltpu.make_async_remote_copy(
            own_ref, sink_ref.at[r - 1], tm_send.at[r - 1], tm_recv.at[r - 1],
            device_id=((tm + r) % times, me), device_id_type=MESH,
        )

    def own_copy(r):
        target = mate if r == 0 else (chip + r) % chips * 2 + core
        return pltpu.make_async_remote_copy(
            own_ref, full_ref.at[me], own_send.at[r], own_recv.at[r],
            device_id=(tm, target), device_id_type=MESH,
        )

    def forward(r):
        slot = (chip + chips - r) % chips * 2 + core
        return pltpu.make_async_remote_copy(
            full_ref.at[slot], full_ref.at[slot], fwd_send.at[r - 1], fwd_recv.at[r - 1],
            device_id=(tm, mate), device_id_type=MESH,
        )

    for r in range(1, times):
        tm_copy(r).start()
    for r in range(1, chips):
        own_copy(r).start()
    own_copy(0).start()
    full_ref[me] = own_ref[...]

    row = lax.broadcasted_iota(jnp.int32, (half, lanes), 0)
    lane = lax.broadcasted_iota(jnp.int32, (half, lanes), 1)
    spot = lane % nvec
    left = spot < half
    real = lane < nvec
    minus_plus = jnp.where(lax.broadcasted_iota(jnp.int32, (nvec, lanes), 1) < nvec, -1.0, 1.0)

    def dense(p):
        t = jnp.transpose(jnp.concatenate([p] * (lanes // half), axis=0))
        base = jnp.where(real, t[:half], t[nvec:nvec + half])
        mixed = jnp.where(real, t[half:nvec], t[nvec + half:])
        moved = pltpu.roll(p, lanes - half, 1)
        zero = jnp.zeros_like(p)
        upper = jnp.where(spot > row, moved, jnp.where(spot < row, -mixed, zero))
        lower = jnp.where(spot - half < row, p, jnp.where(spot - half > row, -mixed, zero))
        return jnp.where(left, upper, -base), jnp.where(left, p, lower)

    def weave(ref):
        even = ref[pl.ds(0, half, stride=2), :]
        odd = ref[pl.ds(1, half, stride=2), :]
        return (
            jnp.where(real, even, pltpu.roll(odd, nvec, 1)),
            jnp.where(real, pltpu.roll(even, nvec, 1), odd),
        )

    for j in range(own):
        top, bottom = dense(own_ref[pl.ds(j, half, stride=own), :])
        board[0:half, :] = -top
        board[half:nvec, :] = -bottom
        even, odd = weave(board)
        out_ref[j, pl.ds(0, half, stride=2), :] = even
        out_ref[j, pl.ds(1, half, stride=2), :] = odd

    combos = spin_ref.shape[0]
    for s in range(combos):
        for q in range(3):
            board[...] = mats_ref[spin_ref[s, q]]
            even, odd = weave(board)
            spin_mats[s, q, pl.ds(0, half, stride=2), :] = even
            spin_mats[s, q, pl.ds(1, half, stride=2), :] = odd
    for s in range(combos):
        for q in range(2):
            spins = spin_mats[s, 2 * q]
            at = (s * 2 + q) * lanes
            top_hi, top_lo = halves(spins)
            low_hi, low_lo = halves(-minus_plus * pltpu.roll(spins, nvec, 1))
            right_hi[0:nvec, at:at + lanes] = top_hi
            right_lo[0:nvec, at:at + lanes] = top_lo
            right_hi[nvec:lanes, at:at + lanes] = low_hi
            right_lo[nvec:lanes, at:at + lanes] = low_lo

    def dot3(a_hi, a_lo, b_hi, b_lo):
        def dot(a, b):
            return jnp.dot(a, b, preferred_element_type=jnp.float32)

        return dot(a_hi, b_hi) + (dot(a_hi, b_lo) + dot(a_lo, b_hi))

    for r in range(1, times):
        tm_copy(r).wait_recv()
    chosen[...] = sink_ref[jnp.clip(times - 1 - shift_ref[0], 0, times - 2)]
    for j in range(own):
        top, bottom = dense(chosen[pl.ds(j, half, stride=own), :])
        hi, lo = halves(jnp.concatenate([top, bottom], axis=0))
        got = dot3(hi, lo, right_hi[...], right_lo[...])
        hi, lo = halves(got)
        for s in range(combos):
            for q in range(2):
                at = (s * 2 + q) * lanes
                where = (s, pl.ds(q * nvec, nvec), pl.ds(j * lanes, lanes))
                half_hi[where] = hi[:, at:at + lanes]
                half_lo[where] = lo[:, at:at + lanes]
    for r in range(1, chips):
        own_copy(r).wait_recv()
        forward(r).start()
    for s in range(combos):
        both = jnp.concatenate(
            [spin_mats[s, 2], spin_mats[s, 0]], axis=0
        )
        hi, lo = halves(jnp.transpose(both))
        got = dot3(hi, lo, half_hi[s], half_lo[s])
        for j in range(own):
            at = j * lanes
            whole = got[:nvec, at:at + lanes] + minus_plus * pltpu.roll(
                got[nvec:, at:at + lanes], nvec, 1
            )
            bent = jnp.where(
                jnp.logical_or(left, spot - half < row),
                whole[half:], pltpu.roll(whole[:half], half, 1),
            )
            weight[pl.ds((s * own + j) * half, half), :] = bent

    mid = []
    for s in range(combos):
        if own % 8 == 0:
            mid.append(spin_mats[s, 1, pl.ds(pl.multiple_of(me * own, own), own), :])
        else:
            for r in range(own):
                mid.append(spin_mats[s, 1, pl.ds(me * own + r, 1), :])
    mid = jnp.concatenate(mid, axis=0)
    count = combos * own
    mid = jnp.concatenate([mid[:, :nvec], pltpu.roll(mid, nvec, 1)[:, :nvec]], axis=0)
    mid_hi, mid_lo = halves(mid)
    own_copy(0).wait_recv()
    for r in range(1, chips):
        forward(r).wait_recv()
    sign = jnp.where(lax.broadcasted_iota(jnp.int32, (count, lanes), 1) < nvec, -1.0, 1.0)
    for k in range(half):
        pieces = [full_ref[d, k * own:(k + 1) * own, :] for d in range(n)]
        hi, lo = halves(jnp.concatenate(pieces, axis=0))
        got = dot3(mid_hi, mid_lo, hi, lo)
        mixed_rows[pl.ds(k * count, count), :] = got[:count] + sign * pltpu.roll(got[count:], nvec, 1)

    straight, crossed = [], []
    for s in range(combos):
        one = jnp.zeros((half, lanes), jnp.float32)
        two = jnp.zeros((half, lanes), jnp.float32)
        for j in range(own):
            at = s * own + j
            value = mixed_rows[pl.ds(at, half, stride=count), :]
            factor = weight[pl.ds(at * half, half), :]
            one = one + value * factor
            two = two + value * pltpu.roll(factor, nvec, 1)
        straight.append(jnp.sum(jnp.where(real, one, -one), axis=0, keepdims=True))
        crossed.append(jnp.sum(two, axis=0, keepdims=True))
    tile_ref[...] = jnp.concatenate(straight + crossed, axis=0)

    def sum_copy(r):
        return pltpu.make_async_remote_copy(
            tile_ref, box.at[r - 1], sum_send.at[r - 1], sum_recv.at[r - 1],
            device_id=(tm, (me + r) % n), device_id_type=MESH,
        )

    for r in range(1, n):
        sum_copy(r).start()
    for s in range(chips):
        pair_copy(s).wait_send()
    for s in range(chips - 1):
        chip_copy(s).wait_send()
    for r in range(1, times):
        tm_copy(r).wait_send()
    own_copy(0).wait_send()
    for r in range(1, chips):
        own_copy(r).wait_send()
        forward(r).wait_send()
    answer = tile_ref[...]
    for r in range(1, n):
        sum_copy(r).wait_recv()
        answer = answer + box[r - 1]
    lines = jnp.sum(answer, axis=1, keepdims=True) * corr_scale
    corr_ref[...] = jnp.concatenate([lines[:combos], lines[combos:]], axis=1)
    for r in range(1, n):
        sum_copy(r).wait_send()


def shards(vectors, perambulators, shift_steps, spin_choice):
    vec = vectors[0]
    _, _, nvec, sites = vec.shape
    spin_pairs = perambulators.shape[1]
    combos = spin_choice.shape[0]
    n = lax.axis_size("space")
    times = lax.axis_size("tm")
    own, half, lanes = nvec // n, nvec // 2, 2 * nvec
    chips = n // 2
    scale = 1.0 / math.sqrt(24.0 * sites * n)
    corr_scale = 0.25 / (nvec * math.sqrt(nvec))
    mats = perambulators[0].reshape(spin_pairs, 2, half, lanes)
    mats = jnp.transpose(mats, (0, 2, 1, 3)).reshape(spin_pairs, nvec, lanes)
    tile = (half * own, lanes)
    f32, bf16 = jnp.float32, jnp.bfloat16
    dma = pltpu.SemaphoreType.DMA
    smem = pl.BlockSpec(memory_space=pltpu.SMEM)
    out, correlator = pl.pallas_call(
        functools.partial(elementals_kernel, n, times, scale, corr_scale),
        out_shape=(
            jax.ShapeDtypeStruct((own, nvec, lanes), f32),
            jax.ShapeDtypeStruct((combos, 2), f32),
        ),
        in_specs=[VM, VM, smem, smem],
        out_specs=(VM, VM),
        scratch_shapes=[
            pltpu.VMEM(tile, f32),
            pltpu.VMEM((n,) + tile, f32),
            pltpu.VMEM((times - 1,) + tile, f32),
            pltpu.VMEM((2, 4 * nvec, 6 * sites), bf16),
            pltpu.VMEM((2, half * own, 6 * sites), bf16),
            pltpu.VMEM((2, half * own, 6 * sites), bf16),
            pltpu.VMEM((chips,) + tile, f32),
            pltpu.VMEM((chips,) + tile, f32),
            pltpu.VMEM((chips,) + tile, f32),
            pltpu.VMEM((chips - 1,) + tile, f32),
            pltpu.VMEM((lanes, combos * 2 * lanes), bf16),
            pltpu.VMEM((lanes, combos * 2 * lanes), bf16),
            pltpu.VMEM((combos, 2 * nvec, own * lanes), bf16),
            pltpu.VMEM((combos, 2 * nvec, own * lanes), bf16),
            pltpu.VMEM((combos * own * half, lanes), f32),
            pltpu.VMEM((combos * own * half, lanes), f32),
            pltpu.VMEM(tile, f32),
            pltpu.VMEM((nvec, lanes), f32),
            pltpu.VMEM((combos, 3, nvec, lanes), f32),
            pltpu.VMEM((2 * combos, lanes), f32),
            pltpu.VMEM((n - 1, 2 * combos, lanes), f32),
            dma((chips,)), dma((chips,)),
            dma((chips - 1,)), dma((chips - 1,)),
            dma((chips,)), dma((chips,)),
            dma((chips - 1,)), dma((chips - 1,)),
            dma((times - 1,)), dma((times - 1,)),
            dma((n - 1,)), dma((n - 1,)),
        ],
        compiler_params=pltpu.CompilerParams(
            collective_id=0, has_side_effects=True, vmem_limit_bytes=60 * 1024 * 1024
        ),
        name="elementals",
    )(vec, mats, shift_steps, spin_choice)
    out = jnp.transpose(out.reshape(own, half, 2, lanes), (0, 2, 1, 3))
    return (out.reshape(1, own, 2, nvec * nvec), correlator[None])


def solution(mesh):
    placed = (P("tm", None, None, None, "space"), P("tm", None, None, None), P("tm"), P())
    return jax.shard_map(
        shards,
        mesh=mesh,
        in_specs=placed,
        out_specs=(P("tm", "space", None, None), P("tm", None, None)),
        check_vma=False,
    )
```

```python
import functools
import math

import jax
import jax.numpy as jnp
from jax import lax
from jax.experimental import pallas as pl
from jax.experimental.pallas import tpu as pltpu
from jax.sharding import PartitionSpec as P

MESH = pl.DeviceIdType.MESH
VM = pl.BlockSpec(memory_space=pltpu.VMEM)
NT_DIMS = (((1,), (1,)), ((), ()))


def halves(x):
    top = x.astype(jnp.bfloat16)
    return top, (x - top.astype(jnp.float32)).astype(jnp.bfloat16)


def at_space(index):
    return (lax.axis_index("tm"), index)


def elementals_kernel(
    n, times, scale, corr_scale, v_ref, mats_ref, shift_ref, spin_ref, out_ref, corr_ref,
    own_ref, full_ref, sink_ref, lead, d_hi, d_lo, keep, give, pair_in, chip_in,
    right_hi, right_lo, half_hi, half_lo, weight, mixed_rows, chosen, board, spin_mats, tile_ref, box,
    pair_send, pair_recv, chip_send, chip_recv,
    own_send, own_recv, fwd_send, fwd_recv, tm_send, tm_recv,
    sum_send, sum_recv,
):
    me = lax.axis_index("space")
    tm = lax.axis_index("tm")
    chips = n // 2
    chip = me // 2
    core = me % 2
    mate = chip * 2 + 1 - core
    nvec = v_ref.shape[2]
    sites = v_ref.shape[3]
    own = nvec // n
    half = nvec // 2
    lanes = 2 * nvec
    group = 16 // own

    barrier = pltpu.get_barrier_semaphore()
    for r in range(1, n):
        pl.semaphore_signal(barrier, inc=1, device_id=(tm, (me + r) % n), device_id_type=MESH)
    for r in range(1, times):
        pl.semaphore_signal(
            barrier, inc=1, device_id=((tm + r) % times, me), device_id_type=MESH
        )

    for kind in range(2):
        for a in range(3):
            re = v_ref[0, a]
            im = v_ref[1, a]
            if kind == 1:
                re = jnp.concatenate([re[half:], re[:half]], axis=0)
                im = jnp.concatenate([im[half:], im[:half]], axis=0)
            re_hi, re_lo = halves(re)
            im_hi, im_lo = halves(im)
            first = pl.ds(a * sites, sites)
            second = pl.ds((3 + a) * sites, sites)
            lead[kind, 0:nvec, first] = re_hi
            lead[kind, 0:nvec, second] = -im_hi
            lead[kind, nvec:lanes, first] = im_hi
            lead[kind, nvec:lanes, second] = re_hi
            lead[kind, lanes:lanes + nvec, first] = re_lo
            lead[kind, lanes:lanes + nvec, second] = -im_lo
            lead[kind, lanes + nvec:2 * lanes, first] = im_lo
            lead[kind, lanes + nvec:2 * lanes, second] = re_lo

    rows = half * own
    row_of = lax.broadcasted_iota(jnp.int32, (rows, lanes), 0) // own
    place = lax.broadcasted_iota(jnp.int32, (rows, lanes), 1) % nvec
    later = jnp.logical_or(place < half, place - half < row_of)

    def block(dest, out_ref):
        start = pl.multiple_of(dest * own, own)

        def rows_of(c, a):
            if own % 8 == 0:
                return v_ref[c, a, pl.ds(start, own), :]
            single = [v_ref[c, a, pl.ds(start + r, 1), :] for r in range(own)]
            return jnp.concatenate(single, axis=0)

        mine = [[rows_of(c, a) for a in range(3)] for c in range(2)]

        def fill(step, carry):
            base = step * group
            for side in range(2):
                got = []
                for g in range(group):
                    k = side * half + base + g
                    other = [[v_ref[c, a, pl.ds(k, 1), :] for a in range(3)] for c in range(2)]
                    cross = []
                    for a in range(3):
                        b, d = (a + 1) % 3, (a + 2) % 3
                        cross.append(
                            mine[0][b] * other[0][d] - mine[1][b] * other[1][d]
                            - (mine[0][d] * other[0][b] - mine[1][d] * other[1][b])
                        )
                    for a in range(3):
                        b, d = (a + 1) % 3, (a + 2) % 3
                        cross.append(
                            mine[0][b] * other[1][d] + mine[1][b] * other[0][d]
                            - (mine[0][d] * other[1][b] + mine[1][d] * other[0][b])
                        )
                    got.append(cross)
                at = pl.ds(pl.multiple_of(base * own, 16), 16)
                for m in range(6):
                    hi, lo = halves(jnp.concatenate([g[m] for g in got], axis=0))
                    d_hi[side, at, m * sites:(m + 1) * sites] = hi
                    d_lo[side, at, m * sites:(m + 1) * sites] = lo
            return carry

        lax.fori_loop(0, half // group, fill, 0)
        sums = []
        for side in range(2):
            kind = 1 - side
            both = lax.dot_general(
                d_hi[side], lead[kind], NT_DIMS, preferred_element_type=jnp.float32
            )
            rest = lax.dot_general(
                d_lo[side], lead[kind, 0:lanes], NT_DIMS, preferred_element_type=jnp.float32
            )
            sums.append(both[:, :lanes] + (both[:, lanes:] + rest))
        out_ref[...] = jnp.where(later, sums[1], sums[0])

    def pair_copy(s):
        return pltpu.make_async_remote_copy(
            give.at[s], pair_in.at[s], pair_send.at[s], pair_recv.at[s],
            device_id=(tm, mate), device_id_type=MESH,
        )

    def chip_copy(s):
        return pltpu.make_async_remote_copy(
            keep.at[s], chip_in.at[s], chip_send.at[s], chip_recv.at[s],
            device_id=(tm, (chip + 1 + s) % chips * 2 + core), device_id_type=MESH,
        )

    def give_block(s):
        block((chip + 1 + s) % chips * 2 + 1 - core, give.at[s])

    def one_chip(s, carry):
        pair_copy(s).start()
        block((chip + 1 + s) % chips * 2 + core, keep.at[s])
        pair_copy(s).wait_recv()
        keep[s] = keep[s] + pair_in[s]

        @pl.when(s < chips - 1)
        def _():
            chip_copy(s).start()
            give_block(s + 1)

        return carry

    give_block(0)
    pl.semaphore_wait(barrier, n - 1 + times - 1)
    lax.fori_loop(0, chips, one_chip, 0)
    row = lax.broadcasted_iota(jnp.int32, (half, lanes), 0)
    lane = lax.broadcasted_iota(jnp.int32, (half, lanes), 1)
    spot = lane % nvec
    left = spot < half
    real = lane < nvec
    minus_plus = jnp.where(lax.broadcasted_iota(jnp.int32, (nvec, lanes), 1) < nvec, -1.0, 1.0)

    def weave(ref):
        even = ref[pl.ds(0, half, stride=2), :]
        odd = ref[pl.ds(1, half, stride=2), :]
        return (
            jnp.where(real, even, pltpu.roll(odd, nvec, 1)),
            jnp.where(real, pltpu.roll(even, nvec, 1), odd),
        )

    combos = spin_ref.shape[0]
    for s in range(combos):
        for q in range(3):
            board[...] = mats_ref[spin_ref[s, q]]
            even, odd = weave(board)
            spin_mats[s, q, pl.ds(0, half, stride=2), :] = even
            spin_mats[s, q, pl.ds(1, half, stride=2), :] = odd
    for s in range(combos):
        for q in range(2):
            spins = spin_mats[s, 2 * q]
            at = (s * 2 + q) * lanes
            top_hi, top_lo = halves(spins)
            low_hi, low_lo = halves(-minus_plus * pltpu.roll(spins, nvec, 1))
            right_hi[0:nvec, at:at + lanes] = top_hi
            right_lo[0:nvec, at:at + lanes] = top_lo
            right_hi[nvec:lanes, at:at + lanes] = low_hi
            right_lo[nvec:lanes, at:at + lanes] = low_lo

    total = keep[chips - 1]
    for s in range(chips - 1):
        chip_copy(s).wait_recv()
        total = total + chip_in[s]
    own_ref[...] = total * scale

    def tm_copy(r):
        return pltpu.make_async_remote_copy(
            own_ref, sink_ref.at[r - 1], tm_send.at[r - 1], tm_recv.at[r - 1],
            device_id=((tm + r) % times, me), device_id_type=MESH,
        )

    def own_copy(r):
        target = mate if r == 0 else (chip + r) % chips * 2 + core
        return pltpu.make_async_remote_copy(
            own_ref, full_ref.at[me], own_send.at[r], own_recv.at[r],
            device_id=(tm, target), device_id_type=MESH,
        )

    def forward(r):
        slot = (chip + chips - r) % chips * 2 + core
        return pltpu.make_async_remote_copy(
            full_ref.at[slot], full_ref.at[slot], fwd_send.at[r - 1], fwd_recv.at[r - 1],
            device_id=(tm, mate), device_id_type=MESH,
        )

    for r in range(1, times):
        tm_copy(r).start()
    for r in range(1, chips):
        own_copy(r).start()
    own_copy(0).start()
    full_ref[me] = own_ref[...]

    def dense(p):
        t = jnp.transpose(jnp.concatenate([p] * (lanes // half), axis=0))
        base = jnp.where(real, t[:half], t[nvec:nvec + half])
        mixed = jnp.where(real, t[half:nvec], t[nvec + half:])
        moved = pltpu.roll(p, lanes - half, 1)
        zero = jnp.zeros_like(p)
        upper = jnp.where(spot > row, moved, jnp.where(spot < row, -mixed, zero))
        lower = jnp.where(spot - half < row, p, jnp.where(spot - half > row, -mixed, zero))
        return jnp.where(left, upper, -base), jnp.where(left, p, lower)

    for j in range(own):
        top, bottom = dense(own_ref[pl.ds(j, half, stride=own), :])
        board[0:half, :] = -top
        board[half:nvec, :] = -bottom
        even, odd = weave(board)
        out_ref[j, pl.ds(0, half, stride=2), :] = even
        out_ref[j, pl.ds(1, half, stride=2), :] = odd

    def dot3(a_hi, a_lo, b_hi, b_lo):
        def dot(a, b):
            return jnp.dot(a, b, preferred_element_type=jnp.float32)

        return dot(a_hi, b_hi) + (dot(a_hi, b_lo) + dot(a_lo, b_hi))

    for r in range(1, times):
        tm_copy(r).wait_recv()
    chosen[...] = sink_ref[jnp.clip(times - 1 - shift_ref[0], 0, times - 2)]
    for j in range(own):
        top, bottom = dense(chosen[pl.ds(j, half, stride=own), :])
        hi, lo = halves(jnp.concatenate([top, bottom], axis=0))
        got = dot3(hi, lo, right_hi[...], right_lo[...])
        hi, lo = halves(got)
        for s in range(combos):
            for q in range(2):
                at = (s * 2 + q) * lanes
                where = (s, pl.ds(q * nvec, nvec), pl.ds(j * lanes, lanes))
                half_hi[where] = hi[:, at:at + lanes]
                half_lo[where] = lo[:, at:at + lanes]
    for r in range(1, chips):
        own_copy(r).wait_recv()
        forward(r).start()
    for s in range(combos):
        both = jnp.concatenate(
            [spin_mats[s, 2], spin_mats[s, 0]], axis=0
        )
        hi, lo = halves(jnp.transpose(both))
        got = dot3(hi, lo, half_hi[s], half_lo[s])
        for j in range(own):
            at = j * lanes
            whole = got[:nvec, at:at + lanes] + minus_plus * pltpu.roll(
                got[nvec:, at:at + lanes], nvec, 1
            )
            bent = jnp.where(
                jnp.logical_or(left, spot - half < row),
                whole[half:], pltpu.roll(whole[:half], half, 1),
            )
            weight[pl.ds((s * own + j) * half, half), :] = bent

    mid = []
    for s in range(combos):
        if own % 8 == 0:
            mid.append(spin_mats[s, 1, pl.ds(pl.multiple_of(me * own, own), own), :])
        else:
            for r in range(own):
                mid.append(spin_mats[s, 1, pl.ds(me * own + r, 1), :])
    mid = jnp.concatenate(mid, axis=0)
    count = combos * own
    mid = jnp.concatenate([mid[:, :nvec], pltpu.roll(mid, nvec, 1)[:, :nvec]], axis=0)
    mid_hi, mid_lo = halves(mid)
    own_copy(0).wait_recv()
    for r in range(1, chips):
        forward(r).wait_recv()
    sign = jnp.where(lax.broadcasted_iota(jnp.int32, (count, lanes), 1) < nvec, -1.0, 1.0)
    for k in range(half):
        pieces = [full_ref[d, k * own:(k + 1) * own, :] for d in range(n)]
        hi, lo = halves(jnp.concatenate(pieces, axis=0))
        got = dot3(mid_hi, mid_lo, hi, lo)
        mixed_rows[pl.ds(k * count, count), :] = got[:count] + sign * pltpu.roll(got[count:], nvec, 1)

    straight, crossed = [], []
    for s in range(combos):
        one = jnp.zeros((half, lanes), jnp.float32)
        two = jnp.zeros((half, lanes), jnp.float32)
        for j in range(own):
            at = s * own + j
            value = mixed_rows[pl.ds(at, half, stride=count), :]
            factor = weight[pl.ds(at * half, half), :]
            one = one + value * factor
            two = two + value * pltpu.roll(factor, nvec, 1)
        straight.append(jnp.sum(jnp.where(real, one, -one), axis=0, keepdims=True))
        crossed.append(jnp.sum(two, axis=0, keepdims=True))
    tile_ref[...] = jnp.concatenate(straight + crossed, axis=0)

    def sum_copy(r):
        return pltpu.make_async_remote_copy(
            tile_ref, box.at[r - 1], sum_send.at[r - 1], sum_recv.at[r - 1],
            device_id=(tm, (me + r) % n), device_id_type=MESH,
        )

    for r in range(1, n):
        sum_copy(r).start()
    for s in range(chips):
        pair_copy(s).wait_send()
    for s in range(chips - 1):
        chip_copy(s).wait_send()
    for r in range(1, times):
        tm_copy(r).wait_send()
    own_copy(0).wait_send()
    for r in range(1, chips):
        own_copy(r).wait_send()
        forward(r).wait_send()
    answer = tile_ref[...]
    for r in range(1, n):
        sum_copy(r).wait_recv()
        answer = answer + box[r - 1]
    lines = jnp.sum(answer, axis=1, keepdims=True) * corr_scale
    corr_ref[...] = jnp.concatenate([lines[:combos], lines[combos:]], axis=1)
    for r in range(1, n):
        sum_copy(r).wait_send()


def shards(vectors, perambulators, shift_steps, spin_choice):
    vec = vectors[0]
    _, _, nvec, sites = vec.shape
    spin_pairs = perambulators.shape[1]
    combos = spin_choice.shape[0]
    n = lax.axis_size("space")
    times = lax.axis_size("tm")
    own, half, lanes = nvec // n, nvec // 2, 2 * nvec
    chips = n // 2
    scale = 1.0 / math.sqrt(24.0 * sites * n)
    corr_scale = 0.25 / (nvec * math.sqrt(nvec))
    mats = perambulators[0].reshape(spin_pairs, 2, half, lanes)
    mats = jnp.transpose(mats, (0, 2, 1, 3)).reshape(spin_pairs, nvec, lanes)
    tile = (half * own, lanes)
    f32, bf16 = jnp.float32, jnp.bfloat16
    dma = pltpu.SemaphoreType.DMA
    smem = pl.BlockSpec(memory_space=pltpu.SMEM)
    out, correlator = pl.pallas_call(
        functools.partial(elementals_kernel, n, times, scale, corr_scale),
        out_shape=(
            jax.ShapeDtypeStruct((own, nvec, lanes), f32),
            jax.ShapeDtypeStruct((combos, 2), f32),
        ),
        in_specs=[VM, VM, smem, smem],
        out_specs=(VM, VM),
        scratch_shapes=[
            pltpu.VMEM(tile, f32),
            pltpu.VMEM((n,) + tile, f32),
            pltpu.VMEM((times - 1,) + tile, f32),
            pltpu.VMEM((2, 4 * nvec, 6 * sites), bf16),
            pltpu.VMEM((2, half * own, 6 * sites), bf16),
            pltpu.VMEM((2, half * own, 6 * sites), bf16),
            pltpu.VMEM((chips,) + tile, f32),
            pltpu.VMEM((chips,) + tile, f32),
            pltpu.VMEM((chips,) + tile, f32),
            pltpu.VMEM((chips - 1,) + tile, f32),
            pltpu.VMEM((lanes, combos * 2 * lanes), bf16),
            pltpu.VMEM((lanes, combos * 2 * lanes), bf16),
            pltpu.VMEM((combos, 2 * nvec, own * lanes), bf16),
            pltpu.VMEM((combos, 2 * nvec, own * lanes), bf16),
            pltpu.VMEM((combos * own * half, lanes), f32),
            pltpu.VMEM((combos * own * half, lanes), f32),
            pltpu.VMEM(tile, f32),
            pltpu.VMEM((nvec, lanes), f32),
            pltpu.VMEM((combos, 3, nvec, lanes), f32),
            pltpu.VMEM((2 * combos, lanes), f32),
            pltpu.VMEM((n - 1, 2 * combos, lanes), f32),
            dma((chips,)), dma((chips,)),
            dma((chips - 1,)), dma((chips - 1,)),
            dma((chips,)), dma((chips,)),
            dma((chips - 1,)), dma((chips - 1,)),
            dma((times - 1,)), dma((times - 1,)),
            dma((n - 1,)), dma((n - 1,)),
        ],
        compiler_params=pltpu.CompilerParams(
            collective_id=0, has_side_effects=True, vmem_limit_bytes=60 * 1024 * 1024
        ),
        name="elementals",
    )(vec, mats, shift_steps, spin_choice)
    out = jnp.transpose(out.reshape(own, half, 2, lanes), (0, 2, 1, 3))
    return (out.reshape(1, own, 2, nvec * nvec), correlator[None])


def solution(mesh):
    placed = (P("tm", None, None, None, "space"), P("tm", None, None, None), P("tm"), P())
    return jax.shard_map(
        shards,
        mesh=mesh,
        in_specs=placed,
        out_specs=(P("tm", "space", None, None), P("tm", None, None)),
        check_vma=False,
    )
```

```python
import functools
import math

import jax
import jax.numpy as jnp
from jax import lax
from jax.experimental import pallas as pl
from jax.experimental.pallas import tpu as pltpu
from jax.sharding import PartitionSpec as P

MESH = pl.DeviceIdType.MESH
VM = pl.BlockSpec(memory_space=pltpu.VMEM)
NT_DIMS = (((1,), (1,)), ((), ()))


def halves(x):
    top = x.astype(jnp.bfloat16)
    return top, (x - top.astype(jnp.float32)).astype(jnp.bfloat16)


def at_space(index):
    return (lax.axis_index("tm"), index)


def elementals_kernel(
    n, times, scale, corr_scale, v_ref, mats_ref, shift_ref, spin_ref, out_ref, corr_ref,
    own_ref, full_ref, sink_ref, lead, d_hi, d_lo, keep, give, pair_in, chip_in,
    right_hi, right_lo, half_hi, half_lo, weight, mixed_rows, chosen, board, spin_mats, tile_ref, box,
    pair_send, pair_recv, chip_send, chip_recv,
    own_send, own_recv, line_send, line_recv, fwd_send, fwd_recv, tm_send, tm_recv,
    sum_send, sum_recv,
):
    me = lax.axis_index("space")
    tm = lax.axis_index("tm")
    chips = n // 2
    chip = me // 2
    core = me % 2
    mate = chip * 2 + 1 - core
    nvec = v_ref.shape[2]
    sites = v_ref.shape[3]
    own = nvec // n
    half = nvec // 2
    lanes = 2 * nvec
    group = 16 // own

    barrier = pltpu.get_barrier_semaphore()
    for r in range(1, n):
        pl.semaphore_signal(barrier, inc=1, device_id=(tm, (me + r) % n), device_id_type=MESH)
    for r in range(1, times):
        pl.semaphore_signal(
            barrier, inc=1, device_id=((tm + r) % times, me), device_id_type=MESH
        )

    for kind in range(2):
        for a in range(3):
            re = v_ref[0, a]
            im = v_ref[1, a]
            if kind == 1:
                re = jnp.concatenate([re[half:], re[:half]], axis=0)
                im = jnp.concatenate([im[half:], im[:half]], axis=0)
            re_hi, re_lo = halves(re)
            im_hi, im_lo = halves(im)
            first = pl.ds(a * sites, sites)
            second = pl.ds((3 + a) * sites, sites)
            lead[kind, 0:nvec, first] = re_hi
            lead[kind, 0:nvec, second] = -im_hi
            lead[kind, nvec:lanes, first] = im_hi
            lead[kind, nvec:lanes, second] = re_hi
            lead[kind, lanes:lanes + nvec, first] = re_lo
            lead[kind, lanes:lanes + nvec, second] = -im_lo
            lead[kind, lanes + nvec:2 * lanes, first] = im_lo
            lead[kind, lanes + nvec:2 * lanes, second] = re_lo

    rows = half * own
    row_of = lax.broadcasted_iota(jnp.int32, (rows, lanes), 0) // own
    place = lax.broadcasted_iota(jnp.int32, (rows, lanes), 1) % nvec
    later = jnp.logical_or(place < half, place - half < row_of)

    def block(dest, out_ref):
        start = pl.multiple_of(dest * own, own)

        def rows_of(c, a):
            if own % 8 == 0:
                return v_ref[c, a, pl.ds(start, own), :]
            single = [v_ref[c, a, pl.ds(start + r, 1), :] for r in range(own)]
            return jnp.concatenate(single, axis=0)

        mine = [[rows_of(c, a) for a in range(3)] for c in range(2)]

        def fill(step, carry):
            base = step * group
            for side in range(2):
                got = []
                for g in range(group):
                    k = side * half + base + g
                    other = [[v_ref[c, a, pl.ds(k, 1), :] for a in range(3)] for c in range(2)]
                    cross = []
                    for a in range(3):
                        b, d = (a + 1) % 3, (a + 2) % 3
                        cross.append(
                            mine[0][b] * other[0][d] - mine[1][b] * other[1][d]
                            - (mine[0][d] * other[0][b] - mine[1][d] * other[1][b])
                        )
                    for a in range(3):
                        b, d = (a + 1) % 3, (a + 2) % 3
                        cross.append(
                            mine[0][b] * other[1][d] + mine[1][b] * other[0][d]
                            - (mine[0][d] * other[1][b] + mine[1][d] * other[0][b])
                        )
                    got.append(cross)
                at = pl.ds(pl.multiple_of(base * own, 16), 16)
                for m in range(6):
                    hi, lo = halves(jnp.concatenate([g[m] for g in got], axis=0))
                    d_hi[side, at, m * sites:(m + 1) * sites] = hi
                    d_lo[side, at, m * sites:(m + 1) * sites] = lo
            return carry

        lax.fori_loop(0, half // group, fill, 0)
        sums = []
        for side in range(2):
            kind = 1 - side
            both = lax.dot_general(
                d_hi[side], lead[kind], NT_DIMS, preferred_element_type=jnp.float32
            )
            rest = lax.dot_general(
                d_lo[side], lead[kind, 0:lanes], NT_DIMS, preferred_element_type=jnp.float32
            )
            sums.append(both[:, :lanes] + (both[:, lanes:] + rest))
        out_ref[...] = jnp.where(later, sums[1], sums[0])

    def pair_copy(s):
        return pltpu.make_async_remote_copy(
            give.at[s], pair_in.at[s], pair_send.at[s], pair_recv.at[s],
            device_id=(tm, mate), device_id_type=MESH,
        )

    def chip_copy(s):
        return pltpu.make_async_remote_copy(
            keep.at[s], chip_in.at[s], chip_send.at[s], chip_recv.at[s],
            device_id=(tm, (chip + 1 + s) % chips * 2 + core), device_id_type=MESH,
        )

    def give_block(s):
        block((chip + 1 + s) % chips * 2 + 1 - core, give.at[s])

    def one_chip(s, carry):
        pair_copy(s).start()
        block((chip + 1 + s) % chips * 2 + core, keep.at[s])
        pair_copy(s).wait_recv()
        keep[s] = keep[s] + pair_in[s]

        @pl.when(s < chips - 1)
        def _():
            chip_copy(s).start()
            give_block(s + 1)

        return carry

    give_block(0)
    pl.semaphore_wait(barrier, n - 1 + times - 1)
    lax.fori_loop(0, chips, one_chip, 0)
    row = lax.broadcasted_iota(jnp.int32, (half, lanes), 0)
    lane = lax.broadcasted_iota(jnp.int32, (half, lanes), 1)
    spot = lane % nvec
    left = spot < half
    real = lane < nvec
    minus_plus = jnp.where(lax.broadcasted_iota(jnp.int32, (nvec, lanes), 1) < nvec, -1.0, 1.0)

    def weave(ref):
        even = ref[pl.ds(0, half, stride=2), :]
        odd = ref[pl.ds(1, half, stride=2), :]
        return (
            jnp.where(real, even, pltpu.roll(odd, nvec, 1)),
            jnp.where(real, pltpu.roll(even, nvec, 1), odd),
        )

    combos = spin_ref.shape[0]
    for s in range(combos):
        for q in range(3):
            board[...] = mats_ref[spin_ref[s, q]]
            even, odd = weave(board)
            spin_mats[s, q, pl.ds(0, half, stride=2), :] = even
            spin_mats[s, q, pl.ds(1, half, stride=2), :] = odd
    for s in range(combos):
        for q in range(2):
            spins = spin_mats[s, 2 * q]
            at = (s * 2 + q) * lanes
            top_hi, top_lo = halves(spins)
            low_hi, low_lo = halves(-minus_plus * pltpu.roll(spins, nvec, 1))
            right_hi[0:nvec, at:at + lanes] = top_hi
            right_lo[0:nvec, at:at + lanes] = top_lo
            right_hi[nvec:lanes, at:at + lanes] = low_hi
            right_lo[nvec:lanes, at:at + lanes] = low_lo

    total = keep[chips - 1]
    for s in range(chips - 1):
        chip_copy(s).wait_recv()
        total = total + chip_in[s]
    own_ref[...] = total * scale

    def tm_copy(r):
        return pltpu.make_async_remote_copy(
            own_ref, sink_ref.at[r - 1], tm_send.at[r - 1], tm_recv.at[r - 1],
            device_id=((tm + r) % times, me), device_id_type=MESH,
        )

    mate_copy = pltpu.make_async_remote_copy(
        own_ref, full_ref.at[me], own_send.at[0], own_recv.at[0],
        device_id=(tm, mate), device_id_type=MESH,
    )

    def slot_of(z):
        return (z + chips) % chips * 2 + core

    def hop(way, t):
        held = slot_of(chip - way * (t - 1))
        side = (1 - way) // 2
        return pltpu.make_async_remote_copy(
            full_ref.at[held], full_ref.at[held],
            line_send.at[side, t - 1], line_recv.at[side, t - 1],
            device_id=(tm, slot_of(chip + way)), device_id_type=MESH,
        )

    def to_mate(way, t):
        held = slot_of(chip - way * t)
        side = (1 - way) // 2
        return pltpu.make_async_remote_copy(
            full_ref.at[held], full_ref.at[held],
            fwd_send.at[side, t - 1], fwd_recv.at[side, t - 1],
            device_id=(tm, mate), device_id_type=MESH,
        )

    def has(z):
        return jnp.logical_and(z >= 0, z < chips)

    def sends(way, t):
        return jnp.logical_and(has(chip + way), has(chip - way * (t - 1)))

    def each_send(t, act):
        for way in (1, -1):
            pl.when(sends(way, t))(functools.partial(act, way, t))

    def each_arrival(t, act):
        for way in (1, -1):
            pl.when(has(chip - way * t))(functools.partial(act, way, t))

    def pass_on(t):
        each_arrival(t, lambda way, t: hop(way, t).wait_recv())
        if t + 1 < chips:
            each_send(t + 1, lambda way, t: hop(way, t).start())
        each_arrival(t, lambda way, t: to_mate(way, t).start())

    full_ref[me] = own_ref[...]
    each_send(1, lambda way, t: hop(way, t).start())
    for r in range(1, times):
        tm_copy(r).start()
    mate_copy.start()

    def dense(p):
        t = jnp.transpose(jnp.concatenate([p] * (lanes // half), axis=0))
        base = jnp.where(real, t[:half], t[nvec:nvec + half])
        mixed = jnp.where(real, t[half:nvec], t[nvec + half:])
        moved = pltpu.roll(p, lanes - half, 1)
        zero = jnp.zeros_like(p)
        upper = jnp.where(spot > row, moved, jnp.where(spot < row, -mixed, zero))
        lower = jnp.where(spot - half < row, p, jnp.where(spot - half > row, -mixed, zero))
        return jnp.where(left, upper, -base), jnp.where(left, p, lower)

    for j in range(own):
        top, bottom = dense(own_ref[pl.ds(j, half, stride=own), :])
        board[0:half, :] = -top
        board[half:nvec, :] = -bottom
        even, odd = weave(board)
        out_ref[j, pl.ds(0, half, stride=2), :] = even
        out_ref[j, pl.ds(1, half, stride=2), :] = odd

    pass_on(1)

    def dot3(a_hi, a_lo, b_hi, b_lo):
        def dot(a, b):
            return jnp.dot(a, b, preferred_element_type=jnp.float32)

        return dot(a_hi, b_hi) + (dot(a_hi, b_lo) + dot(a_lo, b_hi))

    for r in range(1, times):
        tm_copy(r).wait_recv()
    chosen[...] = sink_ref[jnp.clip(times - 1 - shift_ref[0], 0, times - 2)]
    for j in range(own):
        top, bottom = dense(chosen[pl.ds(j, half, stride=own), :])
        hi, lo = halves(jnp.concatenate([top, bottom], axis=0))
        got = dot3(hi, lo, right_hi[...], right_lo[...])
        hi, lo = halves(got)
        for s in range(combos):
            for q in range(2):
                at = (s * 2 + q) * lanes
                where = (s, pl.ds(q * nvec, nvec), pl.ds(j * lanes, lanes))
                half_hi[where] = hi[:, at:at + lanes]
                half_lo[where] = lo[:, at:at + lanes]
        if j == own // 2 - 1:
            pass_on(2)
    for t in range(3, chips):
        pass_on(t)
    for s in range(combos):
        both = jnp.concatenate(
            [spin_mats[s, 2], spin_mats[s, 0]], axis=0
        )
        hi, lo = halves(jnp.transpose(both))
        got = dot3(hi, lo, half_hi[s], half_lo[s])
        for j in range(own):
            at = j * lanes
            whole = got[:nvec, at:at + lanes] + minus_plus * pltpu.roll(
                got[nvec:, at:at + lanes], nvec, 1
            )
            bent = jnp.where(
                jnp.logical_or(left, spot - half < row),
                whole[half:], pltpu.roll(whole[:half], half, 1),
            )
            weight[pl.ds((s * own + j) * half, half), :] = bent

    mid = []
    for s in range(combos):
        if own % 8 == 0:
            mid.append(spin_mats[s, 1, pl.ds(pl.multiple_of(me * own, own), own), :])
        else:
            for r in range(own):
                mid.append(spin_mats[s, 1, pl.ds(me * own + r, 1), :])
    mid = jnp.concatenate(mid, axis=0)
    count = combos * own
    mid = jnp.concatenate([mid[:, :nvec], pltpu.roll(mid, nvec, 1)[:, :nvec]], axis=0)
    mid_hi, mid_lo = halves(mid)
    mate_copy.wait_recv()
    for t in range(1, chips):
        each_arrival(t, lambda way, t: to_mate(way, t).wait_recv())
    sign = jnp.where(lax.broadcasted_iota(jnp.int32, (count, lanes), 1) < nvec, -1.0, 1.0)
    for k in range(half):
        pieces = [full_ref[d, k * own:(k + 1) * own, :] for d in range(n)]
        hi, lo = halves(jnp.concatenate(pieces, axis=0))
        got = dot3(mid_hi, mid_lo, hi, lo)
        mixed_rows[pl.ds(k * count, count), :] = got[:count] + sign * pltpu.roll(got[count:], nvec, 1)

    straight, crossed = [], []
    for s in range(combos):
        one = jnp.zeros((half, lanes), jnp.float32)
        two = jnp.zeros((half, lanes), jnp.float32)
        for j in range(own):
            at = s * own + j
            value = mixed_rows[pl.ds(at, half, stride=count), :]
            factor = weight[pl.ds(at * half, half), :]
            one = one + value * factor
            two = two + value * pltpu.roll(factor, nvec, 1)
        straight.append(jnp.sum(jnp.where(real, one, -one), axis=0, keepdims=True))
        crossed.append(jnp.sum(two, axis=0, keepdims=True))
    tile_ref[...] = jnp.concatenate(straight + crossed, axis=0)

    def sum_copy(r):
        return pltpu.make_async_remote_copy(
            tile_ref, box.at[r - 1], sum_send.at[r - 1], sum_recv.at[r - 1],
            device_id=(tm, (me + r) % n), device_id_type=MESH,
        )

    for r in range(1, n):
        sum_copy(r).start()
    for s in range(chips):
        pair_copy(s).wait_send()
    for s in range(chips - 1):
        chip_copy(s).wait_send()
    for r in range(1, times):
        tm_copy(r).wait_send()
    mate_copy.wait_send()
    for t in range(1, chips):
        each_send(t, lambda way, t: hop(way, t).wait_send())
        each_arrival(t, lambda way, t: to_mate(way, t).wait_send())
    answer = tile_ref[...]
    for r in range(1, n):
        sum_copy(r).wait_recv()
        answer = answer + box[r - 1]
    lines = jnp.sum(answer, axis=1, keepdims=True) * corr_scale
    corr_ref[...] = jnp.concatenate([lines[:combos], lines[combos:]], axis=1)
    for r in range(1, n):
        sum_copy(r).wait_send()


def shards(vectors, perambulators, shift_steps, spin_choice):
    vec = vectors[0]
    _, _, nvec, sites = vec.shape
    spin_pairs = perambulators.shape[1]
    combos = spin_choice.shape[0]
    n = lax.axis_size("space")
    times = lax.axis_size("tm")
    own, half, lanes = nvec // n, nvec // 2, 2 * nvec
    chips = n // 2
    scale = 1.0 / math.sqrt(24.0 * sites * n)
    corr_scale = 0.25 / (nvec * math.sqrt(nvec))
    mats = perambulators[0].reshape(spin_pairs, 2, half, lanes)
    mats = jnp.transpose(mats, (0, 2, 1, 3)).reshape(spin_pairs, nvec, lanes)
    tile = (half * own, lanes)
    f32, bf16 = jnp.float32, jnp.bfloat16
    dma = pltpu.SemaphoreType.DMA
    smem = pl.BlockSpec(memory_space=pltpu.SMEM)
    out, correlator = pl.pallas_call(
        functools.partial(elementals_kernel, n, times, scale, corr_scale),
        out_shape=(
            jax.ShapeDtypeStruct((own, nvec, lanes), f32),
            jax.ShapeDtypeStruct((combos, 2), f32),
        ),
        in_specs=[VM, VM, smem, smem],
        out_specs=(VM, VM),
        scratch_shapes=[
            pltpu.VMEM(tile, f32),
            pltpu.VMEM((n,) + tile, f32),
            pltpu.VMEM((times - 1,) + tile, f32),
            pltpu.VMEM((2, 4 * nvec, 6 * sites), bf16),
            pltpu.VMEM((2, half * own, 6 * sites), bf16),
            pltpu.VMEM((2, half * own, 6 * sites), bf16),
            pltpu.VMEM((chips,) + tile, f32),
            pltpu.VMEM((chips,) + tile, f32),
            pltpu.VMEM((chips,) + tile, f32),
            pltpu.VMEM((chips - 1,) + tile, f32),
            pltpu.VMEM((lanes, combos * 2 * lanes), bf16),
            pltpu.VMEM((lanes, combos * 2 * lanes), bf16),
            pltpu.VMEM((combos, 2 * nvec, own * lanes), bf16),
            pltpu.VMEM((combos, 2 * nvec, own * lanes), bf16),
            pltpu.VMEM((combos * own * half, lanes), f32),
            pltpu.VMEM((combos * own * half, lanes), f32),
            pltpu.VMEM(tile, f32),
            pltpu.VMEM((nvec, lanes), f32),
            pltpu.VMEM((combos, 3, nvec, lanes), f32),
            pltpu.VMEM((2 * combos, lanes), f32),
            pltpu.VMEM((n - 1, 2 * combos, lanes), f32),
            dma((chips,)), dma((chips,)),
            dma((chips - 1,)), dma((chips - 1,)),
            dma((1,)), dma((1,)),
            dma((2, chips - 1)), dma((2, chips - 1)),
            dma((2, chips - 1)), dma((2, chips - 1)),
            dma((times - 1,)), dma((times - 1,)),
            dma((n - 1,)), dma((n - 1,)),
        ],
        compiler_params=pltpu.CompilerParams(
            collective_id=0, has_side_effects=True, vmem_limit_bytes=60 * 1024 * 1024
        ),
        name="elementals",
    )(vec, mats, shift_steps, spin_choice)
    out = jnp.transpose(out.reshape(own, half, 2, lanes), (0, 2, 1, 3))
    return (out.reshape(1, own, 2, nvec * nvec), correlator[None])


def solution(mesh):
    placed = (P("tm", None, None, None, "space"), P("tm", None, None, None), P("tm"), P())
    return jax.shard_map(
        shards,
        mesh=mesh,
        in_specs=placed,
        out_specs=(P("tm", "space", None, None), P("tm", None, None)),
        check_vma=False,
    )
```
